512 devices in a mesh: seq: 256 (over z, y, x), head: 2 (over core).
Axes of the slice: x: 4, y: 8, z: 8, core: 2. Of those that a mesh axis runs over, the one named last changes fastest.
Arguments:
- tokens: bfloat16 [65536, 1024], P(('seq', 'head')), may hold values from -30 to 30
- ln1_gain: float32 [1024], replicated, may hold values from 0.5 to 1.5
- ln1_bias: float32 [1024], replicated, may hold values from -3 to 3
- w_qkv: bfloat16 [1024, 3, 1024], P(None, None, 'head'), may hold values from -1 to 1
- w_out: bfloat16 [1024, 1024], P('head'), may hold values from -0.1875 to 0.1875
- ln2_gain: float32 [1024], replicated, may hold values from 0.5 to 1.5
- ln2_bias: float32 [1024], replicated, may hold values from -3 to 3
- w_up: bfloat16 [1024, 4096], P(None, 'head'), may hold values from -0.1875 to 0.1875
- w_down: bfloat16 [4096, 1024], P('head'), may hold values from -0.09375 to 0.09375
- block_mask: int32 [256, 256], replicated, may hold values from 0 to 1, as said below
Outputs:
- layer_out: bfloat16 [65536, 1024], P(('seq', 'head'))
The draws below stay inside these ranges and needn't reach their ends.
Inputs may be any that keep to these rules, and one draw needn't show every extreme that they name: `block_mask`: the diagonal is 1; every 1 lies within 4 blocks of the diagonal; each row holds 2 to 8 ones, and some row holds exactly 8.
All inputs are finite; a program needn't handle non-finite values.
Results may differ from the reference program's by a relative error of at most 0.0095.
Values may be sent and summed in bfloat16 or wider, within the bound.
No kernel may reach another device: no remote copies, remote signals or barrier semaphores. Data moves between devices by JAX's collectives and lax.ppermute only.
A program may use at most 64 MiB of HBM per device.

```python
import math
import jax
import jax.numpy as jnp
from jax import lax

D = 1024
HEADS = 16
HDIM = 64
FF = 4096
KMAX = 8
REACH = 4
BLK = 256
NBLK = 256
TOKENS = 65536


def draw_tokens(key, part):
    base = jnp.clip(jax.random.normal(jax.random.fold_in(key, 1), (TOKENS, D), jnp.float32), -3.0, 3.0)
    row_scale = jnp.exp(jax.random.uniform(jax.random.fold_in(key, 2), (TOKENS, 1), jnp.float32, math.log(0.3), math.log(3.0)))
    col_scale = jnp.exp(jax.random.uniform(jax.random.fold_in(key, 3), (1, D), jnp.float32, math.log(0.3), math.log(3.0)))
    return (base * row_scale * col_scale).astype(jnp.bfloat16)


def draw_w_qkv(key, part):
    base = jnp.clip(jax.random.normal(jax.random.fold_in(key, 5), (D, 3, D), jnp.float32), -4.0, 4.0) / math.sqrt(D)
    return jnp.clip(base, -1.0, 1.0).astype(jnp.bfloat16)


def draw_block_mask(key, part):
    index = jnp.arange(NBLK, dtype=jnp.int32)
    reach_count = jnp.minimum(index, REACH) + jnp.minimum(NBLK - 1 - index, REACH)
    eligible = reach_count >= KMAX - 1
    ranking = jax.random.permutation(jax.random.fold_in(key, 11), NBLK).astype(jnp.int32)
    keyed = jnp.where(eligible, ranking, ranking + NBLK)
    chosen = jnp.argmin(keyed).astype(jnp.int32)
    heavy = eligible & ((ranking < max(1, NBLK // 8)) | (index == chosen))
    light = jax.random.randint(jax.random.fold_in(key, 12), (NBLK,), 1, 4, jnp.int32)
    wanted = jnp.where(heavy, KMAX - 1, jnp.minimum(light, reach_count))
    offsets = index[:, None] - index[None, :]
    nearby = (jnp.abs(offsets) <= REACH) & (offsets != 0)
    priority = jax.random.randint(jax.random.fold_in(key, 13), (NBLK, NBLK), 0, 4096, jnp.int32) * NBLK + index[None, :]
    priority = jnp.where(nearby, priority, -1)
    higher = jnp.sum((priority[:, None, :] > priority[:, :, None]).astype(jnp.int32), axis=2)
    picked = nearby & (higher < wanted[:, None])
    return (picked | (offsets == 0)).astype(jnp.int32)


def block_levels(stream_key, extent, split, smallest, high):
    factor_of, own = 1.0, jax.random.fold_in(stream_key, 6)
    for axis_at, shards_of in split:
        heights = jnp.exp(jax.random.uniform(jax.random.fold_in(own, axis_at), (shards_of,), jnp.float32, smallest / len(split), high / len(split)))
        factor_of = factor_of * jnp.repeat(heights, extent[axis_at] // shards_of).reshape([-1 if axis == axis_at else 1 for axis in range(len(extent))])
    return factor_of


def centred(own_key, dims, deviation, limit, cuts=(), held_as=jnp.bfloat16):
    level = block_levels(own_key, dims, cuts, -0.22, 0.18) if cuts else 1.0
    drawn = jax.random.normal(own_key, dims, jnp.float32) * deviation * level
    return jnp.minimum(jnp.maximum(drawn, -limit), limit).astype(held_as)


def setup_inputs(seed: int = 0) -> dict:
    streams_of = jax.random.split(jax.random.key(seed), 11)
    return {
        "tokens": draw_tokens(jax.random.fold_in(streams_of[10], 71), 0),
        "ln1_gain": jnp.clip(1.0 + 0.1 * jax.random.normal(streams_of[1], (D,), jnp.float32), 0.5, 1.5),
        "ln1_bias": centred(streams_of[2], (D,), 0.5, 3.0, (), jnp.float32),
        "w_qkv": draw_w_qkv(jax.random.fold_in(streams_of[10], 71), 0),
        "w_out": centred(streams_of[4], (D, D), D ** -0.5, 0.1875, ((0, 2),)),
        "ln2_gain": jnp.clip(1.0 + 0.1 * jax.random.normal(streams_of[5], (D,), jnp.float32), 0.5, 1.5),
        "ln2_bias": centred(streams_of[6], (D,), 0.5, 3.0, (), jnp.float32),
        "w_up": centred(streams_of[7], (D, FF), D ** -0.5, 0.1875, ((1, 2),)),
        "w_down": centred(streams_of[8], (FF, D), FF ** -0.5, 0.09375, ((0, 2),)),
        "block_mask": draw_block_mask(jax.random.fold_in(streams_of[10], 71), 0),
    }


norm_eps = 1e-06

def layer_norm(inputs, gain, shift):
    inputs = inputs.astype(jnp.float32)
    center = inputs - lax.optimization_barrier(jnp.mean(inputs, axis=-1, keepdims=True))
    spread = lax.optimization_barrier(jnp.mean(center * center, axis=-1, keepdims=True))
    return center * lax.rsqrt(spread + norm_eps) * gain.astype(jnp.float32) + shift.astype(jnp.float32)

def attend(states, query_blk, key_blk, value_blk):
    running_max, running_sum, weighted = states
    scores = jnp.einsum('qhd,khd->hqk', query_blk.astype(jnp.float32), key_blk.astype(jnp.float32)) * HDIM ** (-0.5)
    new_max = jnp.maximum(running_max, lax.optimization_barrier(jnp.max(scores, axis=2)))
    decay = jnp.exp(running_max - new_max)
    weights = jnp.exp(scores - new_max[:, :, None])
    running_sum = running_sum * decay + lax.optimization_barrier(jnp.sum(weights, axis=2))
    rounded = lax.optimization_barrier(weights.astype(jnp.bfloat16))
    mixture = jnp.einsum('hqk,khd->qhd', rounded.astype(jnp.float32), value_blk.astype(jnp.float32))
    weighted = weighted * decay.T[:, :, None] + mixture
    return (new_max, running_sum, weighted)

def reference(tokens, ln1_gain, ln1_bias, w_qkv, w_out, ln2_gain, ln2_bias, w_up, w_down, block_mask):
    normed_one = layer_norm(tokens, ln1_gain, ln1_bias).astype(jnp.bfloat16)
    queries = jnp.dot(normed_one, w_qkv[:, 0, :], preferred_element_type=jnp.float32).astype(jnp.bfloat16)
    keys_all = jnp.dot(normed_one, w_qkv[:, 1, :], preferred_element_type=jnp.float32).astype(jnp.bfloat16)
    values = jnp.dot(normed_one, w_qkv[:, 2, :], preferred_element_type=jnp.float32).astype(jnp.bfloat16)
    query_b = queries.reshape(NBLK, BLK, HEADS, HDIM)
    key_b = keys_all.reshape(NBLK, BLK, HEADS, HDIM)
    value_b = values.reshape(NBLK, BLK, HEADS, HDIM)
    order = jnp.argsort(1 - block_mask, axis=1).astype(jnp.int32)[:, :KMAX]
    listed = jnp.take_along_axis(block_mask, order, axis=1)

    def one_block(inputs):
        query_blk, block_ids, flags = inputs
        start = (jnp.full((HEADS, BLK), -1e+30, jnp.float32), jnp.zeros((HEADS, BLK), jnp.float32), jnp.zeros((BLK, HEADS, HDIM), jnp.float32))

        def over_slot(states, slot):
            block_id, flag = slot
            key_blk = lax.dynamic_index_in_dim(key_b, block_id, 0, keepdims=False)
            value_blk = lax.dynamic_index_in_dim(value_b, block_id, 0, keepdims=False)
            states = lax.cond(flag > 0, lambda inner: attend(inner, query_blk, key_blk, value_blk), lambda inner: inner, states)
            return (states, None)
        final, unused = lax.scan(over_slot, start, (block_ids, flags))
        running_max, running_sum, weighted = final
        attended = weighted / running_sum.T[:, :, None]
        return attended.reshape(BLK, D).astype(jnp.bfloat16)
    attended = lax.map(one_block, (query_b, order, listed)).reshape(TOKENS, D)
    resid = (tokens.astype(jnp.float32) + jnp.dot(attended, w_out, preferred_element_type=jnp.float32)).astype(jnp.bfloat16)

    def mlp_block(rows):
        normed_two = layer_norm(rows, ln2_gain, ln2_bias).astype(jnp.bfloat16)
        hidden = jax.nn.gelu(jnp.dot(normed_two, w_up, preferred_element_type=jnp.float32), approximate=False).astype(jnp.bfloat16)
        return (rows.astype(jnp.float32) + jnp.dot(hidden, w_down, preferred_element_type=jnp.float32)).astype(jnp.bfloat16)
    layer_out = lax.map(mlp_block, resid.reshape(NBLK, BLK, D)).reshape(TOKENS, D)
    return layer_out
```

```python
import math

import jax
import jax.numpy as jnp
from jax import lax
from jax.experimental import pallas as pl
from jax.experimental.pallas import tpu as pltpu
from jax.sharding import PartitionSpec as P


HDIM = 64
REACH = 4
LANES = 128
STEP_COLS = 256
EXP_SCALE = HDIM ** (-0.5) * math.log2(math.e)
F32 = jnp.float32
BF16 = jnp.bfloat16

norm_eps = 1e-06


def layer_norm(inputs, gain, shift):
    inputs = inputs.astype(F32)
    center = inputs - jnp.mean(inputs, axis=-1, keepdims=True)
    spread = jnp.mean(center * center, axis=-1, keepdims=True)
    return center * lax.rsqrt(spread + norm_eps) * gain + shift


def dot(left, right):
    return jnp.dot(left, right, preferred_element_type=F32)


def norm_kernel(tokens_ref, gain_ref, bias_ref, out_ref):
    out_ref[...] = layer_norm(tokens_ref[...], gain_ref[...], bias_ref[...]).astype(BF16)


def norm_rows(tokens, gain, bias):
    return pl.pallas_call(
        norm_kernel,
        out_shape=jax.ShapeDtypeStruct(tokens.shape, BF16),
        name="norm_rows",
    )(tokens, gain.reshape(1, -1), bias.reshape(1, -1))


def attend_pair(query_pair, key_pair, value_pair, old_max, old_sum, old_acc):
    rows = query_pair.shape[0]
    first = lax.broadcasted_iota(jnp.int32, (rows, LANES), 1) < HDIM
    zero = jnp.zeros_like(query_pair)
    stacked = jnp.concatenate(
        [jnp.where(first, query_pair, zero), jnp.where(first, zero, query_pair)], axis=0
    )
    scores = (
        lax.dot_general(stacked, key_pair, (((1,), (1,)), ((), ())), preferred_element_type=F32)
        * EXP_SCALE
    )
    new_max = jnp.max(scores, axis=1, keepdims=True)
    if old_max is not None:
        new_max = jnp.maximum(old_max, new_max)
    weights = jnp.exp2(scores - new_max)
    new_sum = jnp.sum(weights, axis=1, keepdims=True)
    mixture = dot(weights.astype(BF16), value_pair)
    mixed = jnp.where(first, mixture[:rows], mixture[rows:])
    if old_max is not None:
        decay = jnp.exp2(old_max - new_max)
        new_sum = new_sum + old_sum * decay
        mixed = mixed + old_acc * jnp.where(first, decay[:rows], decay[rows:])
    return new_max, new_sum, mixed


def attend_step(queries, rows, w_key, w_value, stats_in, acc_in, stats_ref, acc_ref):
    keys = dot(rows, w_key).astype(BF16)
    values = dot(rows, w_value).astype(BF16)
    count = queries.shape[0]
    for pair in range(STEP_COLS // LANES):
        cols = slice(pair * LANES, (pair + 1) * LANES)
        old_max = old_sum = old_acc = None
        if stats_in is not None:
            lane = 4 * pair
            old_max = jnp.concatenate(
                [stats_in[0, :, lane : lane + 1], stats_in[0, :, lane + 1 : lane + 2]], axis=0
            )
            old_sum = jnp.concatenate(
                [stats_in[0, :, lane + 2 : lane + 3], stats_in[0, :, lane + 3 : lane + 4]], axis=0
            )
            old_acc = acc_in[:, cols]
        new_max, new_sum, mixed = attend_pair(
            queries[:, cols], keys[:, cols], values[:, cols], old_max, old_sum, old_acc
        )
        lane = 4 * pair
        stats_ref[0, :, lane : lane + 1] = new_max[:count]
        stats_ref[0, :, lane + 1 : lane + 2] = new_max[count:]
        stats_ref[0, :, lane + 2 : lane + 3] = new_sum[:count]
        stats_ref[0, :, lane + 3 : lane + 4] = new_sum[count:]
        acc_ref[:, cols] = mixed


def own_kernel(
    both_ref, mine_ref, w_own_ref, w_other_ref, query_ref, acc_ref, stats_ref
):
    step = pl.program_id(0)

    def work(weights):
        queries = dot(both_ref[...], weights[0]).astype(BF16)
        query_ref[...] = queries
        attend_step(
            queries, mine_ref[...], weights[1], weights[2], None, None, stats_ref, acc_ref
        )

    half = pl.num_programs(0) // 2

    @pl.when(step < half)
    def _():
        work(w_own_ref)

    @pl.when(step >= half)
    def _():
        work(w_other_ref)


def own_attention(both, mine, w_own, w_other):
    rows, width = both.shape
    steps = width // STEP_COLS
    half = steps // 2
    return pl.pallas_call(
        own_kernel,
        grid=(steps,),
        in_specs=[
            pl.BlockSpec(both.shape, lambda j: (0, 0)),
            pl.BlockSpec(mine.shape, lambda j: (0, 0)),
            pl.BlockSpec((3, width, STEP_COLS), lambda j: (0, 0, jnp.minimum(j, half - 1))),
            pl.BlockSpec((3, width, STEP_COLS), lambda j: (0, 0, jnp.maximum(j - half, 0))),
        ],
        out_specs=[
            pl.BlockSpec((rows, STEP_COLS), lambda j: (0, j)),
            pl.BlockSpec((rows, STEP_COLS), lambda j: (0, j)),
            pl.BlockSpec((1, rows, LANES), lambda j: (j, 0, 0)),
        ],
        out_shape=[
            jax.ShapeDtypeStruct((rows, width), BF16),
            jax.ShapeDtypeStruct((rows, width), F32),
            jax.ShapeDtypeStruct((steps, rows, LANES), F32),
        ],
        name="own_attention",
    )(both, mine, w_own, w_other)


def block_kernel(
    place_ref,
    mask_ref,
    query_ref,
    rows_ref,
    key_own_ref,
    value_own_ref,
    key_other_ref,
    value_other_ref,
    acc_in,
    stats_in,
    acc_ref,
    stats_ref,
    *,
    distance,
    blocks,
):
    step = pl.program_id(0)
    half = pl.num_programs(0) // 2
    here = place_ref[0]
    source = jnp.where(place_ref[1] == 0, here - distance, here + distance)
    inside = (source >= 0) & (source < blocks)
    listed = mask_ref[here % 8, jnp.clip(source, 0, blocks - 1)]
    active = inside & (listed > 0)

    def work(w_key, w_value):
        attend_step(
            query_ref[...], rows_ref[...], w_key[0], w_value[0], stats_in, acc_in, stats_ref, acc_ref
        )

    @pl.when(active & (step < half))
    def _():
        work(key_own_ref, value_own_ref)

    @pl.when(active & (step >= half))
    def _():
        work(key_other_ref, value_other_ref)

    @pl.when(jnp.logical_not(active))
    def _():
        acc_ref[...] = acc_in[...]
        stats_ref[...] = stats_in[...]


def block_attention(place, block_mask, queries, rows, w_own, w_other, acc, stats, distance):
    count, width = queries.shape
    steps = width // STEP_COLS
    half = steps // 2
    blocks = block_mask.shape[0]

    def body(*refs):
        block_kernel(*refs, distance=distance, blocks=blocks)

    grid_spec = pltpu.PrefetchScalarGridSpec(
        num_scalar_prefetch=1,
        grid=(steps,),
        in_specs=[
            pl.BlockSpec((8, blocks), lambda j, s: (s[0] // 8, 0), memory_space=pltpu.SMEM),
            pl.BlockSpec((count, STEP_COLS), lambda j, s: (0, j)),
            pl.BlockSpec(rows.shape, lambda j, s: (0, 0)),
            pl.BlockSpec((1, width, STEP_COLS), lambda j, s: (1, 0, jnp.minimum(j, half - 1))),
            pl.BlockSpec((1, width, STEP_COLS), lambda j, s: (2, 0, jnp.minimum(j, half - 1))),
            pl.BlockSpec((1, width, STEP_COLS), lambda j, s: (1, 0, jnp.maximum(j - half, 0))),
            pl.BlockSpec((1, width, STEP_COLS), lambda j, s: (2, 0, jnp.maximum(j - half, 0))),
            pl.BlockSpec((count, STEP_COLS), lambda j, s: (0, j)),
            pl.BlockSpec((1, count, LANES), lambda j, s: (j, 0, 0)),
        ],
        out_specs=[
            pl.BlockSpec((count, STEP_COLS), lambda j, s: (0, j)),
            pl.BlockSpec((1, count, LANES), lambda j, s: (j, 0, 0)),
        ],
    )
    return pl.pallas_call(
        body,
        grid_spec=grid_spec,
        out_shape=[
            jax.ShapeDtypeStruct(acc.shape, F32),
            jax.ShapeDtypeStruct(stats.shape, F32),
        ],
        input_output_aliases={8: 0, 9: 1},
    )(place, block_mask, queries, rows, w_own, w_own, w_other, w_other, acc, stats)


def pack_kernel(place_ref, acc_ref, stats_ref, out_ref):
    steps = stats_ref.shape[0]
    width = acc_ref.shape[1]
    out_ref[:, :width] = acc_ref[...]
    for j in range(steps):
        out_ref[:, width + 8 * j : width + 8 * j + 8] = stats_ref[j, :, 0:8]
    out_ref[:, width + 8 * steps :] = jnp.zeros(
        (out_ref.shape[0], out_ref.shape[1] - width - 8 * steps), F32
    )


def pack(place, acc, stats):
    count, width = acc.shape
    half = count // 2
    steps = stats.shape[0]
    grid_spec = pltpu.PrefetchScalarGridSpec(
        num_scalar_prefetch=1,
        grid=(1,),
        in_specs=[
            pl.BlockSpec((half, width), lambda i, s: (1 - s[1], 0)),
            pl.BlockSpec((steps, half, LANES), lambda i, s: (0, 1 - s[1], 0)),
        ],
        out_specs=pl.BlockSpec((half, width + LANES), lambda i, s: (0, 0)),
    )
    return pl.pallas_call(
        pack_kernel,
        grid_spec=grid_spec,
        out_shape=jax.ShapeDtypeStruct((half, width + LANES), F32),
        name="pack",
    )(place, acc, stats)


def tail_kernel(
    place_ref,
    acc_ref,
    stats_ref,
    sent_ref,
    tokens_ref,
    w_out_own,
    w_out_other,
    gain_ref,
    bias_ref,
    w_up_own,
    w_up_other,
    w_down_own,
    w_down_other,
    out_ref,
    out_buf,
    up_buf,
    down_buf,
    out_sem,
    up_sem,
    down_sem,
):
    rows, width = tokens_ref.shape
    steps = stats_ref.shape[0]
    half = steps // 2
    chunk = up_buf.shape[2]
    hidden_half = w_up_own.shape[1]
    per_half = hidden_half // chunk

    copies_out = [
        pltpu.make_async_copy(source, out_buf.at[i], out_sem.at[i])
        for i, source in enumerate((w_out_own, w_out_other))
    ]
    copies_up = []
    copies_down = []
    for i, (up, down) in enumerate(((w_up_own, w_down_own), (w_up_other, w_down_other))):
        for j in range(per_half):
            k = i * per_half + j
            copies_up.append(
                pltpu.make_async_copy(
                    up.at[:, pl.ds(j * chunk, chunk)], up_buf.at[k], up_sem.at[k]
                )
            )
            copies_down.append(
                pltpu.make_async_copy(
                    down.at[pl.ds(j * chunk, chunk), :], down_buf.at[k], down_sem.at[k]
                )
            )
    for copy in copies_out:
        copy.start()
    for up, down in zip(copies_up, copies_down):
        up.start()
        down.start()

    first = lax.broadcasted_iota(jnp.int32, (rows, LANES), 1) < HDIM
    pieces = []
    for j in range(steps):
        other = (j + half) % steps
        for pair in range(STEP_COLS // LANES):
            mine = []
            theirs = []
            for head in range(2):
                lane = 4 * pair + head
                base = width + 8 * other + lane
                my_max = stats_ref[j, :, lane : lane + 1]
                my_sum = stats_ref[j, :, lane + 2 : lane + 3]
                their_max = sent_ref[:, base : base + 1]
                their_sum = sent_ref[:, base + 2 : base + 3]
                top = jnp.maximum(my_max, their_max)
                my_part = jnp.exp2(my_max - top)
                their_part = jnp.exp2(their_max - top)
                total = my_sum * my_part + their_sum * their_part
                mine.append(my_part / total)
                theirs.append(their_part / total)
            col = j * STEP_COLS + pair * LANES
            col_other = other * STEP_COLS + pair * LANES
            merged = acc_ref[:, col : col + LANES] * jnp.where(first, mine[0], mine[1])
            merged = merged + sent_ref[:, col_other : col_other + LANES] * jnp.where(
                first, theirs[0], theirs[1]
            )
            pieces.append(merged.astype(BF16))
    attended = jnp.concatenate(pieces, axis=1)
    for copy in copies_out:
        copy.wait()
    halfway = width // 2
    projected = dot(attended[:, :halfway], out_buf[0]) + dot(attended[:, halfway:], out_buf[1])
    resid = (tokens_ref[...].astype(F32) + projected).astype(BF16)
    normed = layer_norm(resid, gain_ref[...], bias_ref[...]).astype(BF16)
    total = resid.astype(F32)
    for k in range(2 * per_half):
        copies_up[k].wait()
        raised = dot(normed, up_buf[k])
        hidden = (raised * (1.0 + lax.erf(raised * (0.5**0.5))) * 0.5).astype(BF16)
        copies_down[k].wait()
        total = total + dot(hidden, down_buf[k])
    out_ref[...] = total.astype(BF16)


def tail(place, acc, stats, both_sent, tokens, w_out, w_out_other, gain, bias, w_up, w_up_other, w_down, w_down_other):
    rows, width = tokens.shape
    steps = stats.shape[0]
    hidden_half = w_up.shape[1]
    chunk = 512
    chunks = 2 * hidden_half // chunk
    whole = pl.BlockSpec(memory_space=pl.ANY)
    vector = pl.BlockSpec((1, width), lambda i, s: (0, 0))
    grid_spec = pltpu.PrefetchScalarGridSpec(
        num_scalar_prefetch=1,
        grid=(1,),
        in_specs=[
            pl.BlockSpec((rows, width), lambda i, s: (s[1], 0)),
            pl.BlockSpec((steps, rows, LANES), lambda i, s: (0, s[1], 0)),
            pl.BlockSpec((rows, width + LANES), lambda i, s: (0, 0)),
            pl.BlockSpec((rows, width), lambda i, s: (0, 0)),
            whole,
            whole,
            vector,
            vector,
            whole,
            whole,
            whole,
            whole,
        ],
        out_specs=pl.BlockSpec((rows, width), lambda i, s: (0, 0)),
        scratch_shapes=[
            pltpu.VMEM((2, width // 2, width), BF16),
            pltpu.VMEM((chunks, width, chunk), BF16),
            pltpu.VMEM((chunks, chunk, width), BF16),
            pltpu.SemaphoreType.DMA((2,)),
            pltpu.SemaphoreType.DMA((chunks,)),
            pltpu.SemaphoreType.DMA((chunks,)),
        ],
    )
    return pl.pallas_call(
        tail_kernel,
        grid_spec=grid_spec,
        out_shape=jax.ShapeDtypeStruct(tokens.shape, BF16),
        name="tail",
    )(
        place,
        acc,
        stats,
        both_sent,
        tokens,
        w_out,
        w_out_other,
        gain.reshape(1, -1),
        bias.reshape(1, -1),
        w_up,
        w_up_other,
        w_down,
        w_down_other,
    )


def from_partner(array):
    return lax.ppermute(array, "head", [(0, 1), (1, 0)])


def from_block(array, distance):
    blocks = lax.axis_size("seq")
    ahead = [(2 * i, 2 * (i + distance)) for i in range(blocks - distance)]
    behind = [(2 * i + 1, 2 * (i - distance) + 1) for i in range(distance, blocks)]
    return lax.ppermute(array, ("seq", "head"), ahead + behind)


def shards(tokens, ln1_gain, ln1_bias, w_qkv, w_out, ln2_gain, ln2_bias, w_up, w_down, block_mask):
    here = lax.axis_index("seq")
    core = lax.axis_index("head")
    place = jnp.stack([here, core]).astype(jnp.int32)
    w_own = jnp.transpose(w_qkv, (1, 0, 2))
    mine = norm_rows(tokens, ln1_gain, ln1_bias)
    both = lax.all_gather(mine, "head", axis=0, tiled=True)
    near = {}
    for d in range(1, REACH + 1):
        near[d] = from_block(both, d)
    w_other = from_partner(w_own)
    w_out_other = from_partner(w_out)
    w_up_other = from_partner(w_up)
    w_down_other = from_partner(w_down)
    queries, acc, stats = own_attention(both, mine, w_own, w_other)
    for d in (1, 3, 4, 2):
        acc, stats = block_attention(
            place, block_mask, queries, near[d], w_own, w_other, acc, stats, d
        )
    packed = pack(place, acc, stats)
    sent = from_partner(packed)
    return tail(
        place,
        acc,
        stats,
        sent,
        tokens,
        w_out,
        w_out_other,
        ln2_gain,
        ln2_bias,
        w_up,
        w_up_other,
        w_down,
        w_down_other,
    )


def solution(mesh):
    in_specs = (
        P(("seq", "head"), None),
        P(),
        P(),
        P(None, None, "head"),
        P("head", None),
        P(),
        P(),
        P(None, "head"),
        P("head", None),
        P(),
    )
    out_specs = P(("seq", "head"), None)
    return jax.shard_map(
        shards, mesh=mesh, in_specs=in_specs, out_specs=out_specs, check_vma=False
    )
```

```python
import math

import jax
import jax.numpy as jnp
from jax import lax
from jax.experimental import pallas as pl
from jax.experimental.pallas import tpu as pltpu
from jax.sharding import PartitionSpec as P


HDIM = 64
REACH = 4
LANES = 128
STEP_COLS = 256
EXP_SCALE = HDIM ** (-0.5) * math.log2(math.e)
F32 = jnp.float32
BF16 = jnp.bfloat16

norm_eps = 1e-06


def layer_norm(inputs, gain, shift):
    inputs = inputs.astype(F32)
    center = inputs - jnp.mean(inputs, axis=-1, keepdims=True)
    spread = jnp.mean(center * center, axis=-1, keepdims=True)
    return center * lax.rsqrt(spread + norm_eps) * gain + shift


def dot(left, right):
    return jnp.dot(left, right, preferred_element_type=F32)


def held(array):
    return pltpu.with_memory_space_constraint(array, pltpu.VMEM)


def in_hbm(array):
    return pltpu.with_memory_space_constraint(array, pltpu.HBM)


def in_vmem():
    return pl.BlockSpec(memory_space=pltpu.VMEM)


def vmem_out(shape, dtype):
    return pltpu.VMEM(shape, dtype)


def params(mib):
    return pltpu.CompilerParams(vmem_limit_bytes=mib * 1024 * 1024)


def norm_kernel(here_ref, core_ref, tokens_ref, gain_ref, bias_ref, out_ref):
    out_ref[...] = layer_norm(tokens_ref[...], gain_ref[...], bias_ref[...]).astype(BF16)


def norm_rows(place, tokens, gain, bias):
    rows, width = tokens.shape
    vector = pl.BlockSpec((1, width), lambda i, s, c: (0, 0))
    whole = pl.BlockSpec((rows, width), lambda i, s, c: (0, 0))
    grid_spec = pltpu.PrefetchScalarGridSpec(
        num_scalar_prefetch=2, grid=(1,), in_specs=[whole, vector, vector], out_specs=whole
    )
    return pl.pallas_call(
        norm_kernel,
        grid_spec=grid_spec,
        out_shape=jax.ShapeDtypeStruct(tokens.shape, BF16),
        name="norm_rows",
    )(*place, tokens, gain.reshape(1, -1), bias.reshape(1, -1))


def attend_heads(keys, values_t, query_ref, pair, acc_ref, stats_ref, fresh):
    count = query_ref.shape[2] // 2
    scores = dot(keys, query_ref[pair])
    top = jnp.max(scores, axis=0, keepdims=True)
    old_top = stats_ref[pair, 0:1, :]
    if not fresh:
        top = jnp.maximum(top, old_top)
    weights = jnp.exp2((scores - top) * EXP_SCALE)
    total = jnp.sum(weights, axis=0, keepdims=True)
    low = weights.astype(BF16)
    if not fresh:
        decay = jnp.exp2((old_top - top) * EXP_SCALE)
        total = total + stats_ref[pair, 1:2, :] * decay
    stats_ref[pair, 0:1, :] = top
    stats_ref[pair, 1:2, :] = total
    for head in range(2):
        lanes = slice(head * count, (head + 1) * count)
        rows = slice((2 * pair + head) * HDIM, (2 * pair + head + 1) * HDIM)
        mixture = dot(values_t[head * HDIM : (head + 1) * HDIM], low[:, lanes])
        if not fresh:
            mixture = mixture + acc_ref[rows, :] * decay[:, lanes]
        acc_ref[rows, :] = mixture


def attend_rows(rows, w_pair, query_ref, acc_ref, stats_ref, fresh):
    per_step = STEP_COLS // LANES
    pair = 0
    for weights in w_pair:
        for start in range(0, weights.shape[2], STEP_COLS):
            cols = slice(start, start + STEP_COLS)
            keys = dot(rows, weights[1, :, cols]).astype(BF16)
            values_t = dot(rows, weights[2, :, cols]).astype(BF16).T
            for i in range(per_step):
                part = slice(i * LANES, (i + 1) * LANES)
                attend_heads(
                    keys[:, part], values_t[part], query_ref, pair, acc_ref, stats_ref, fresh
                )
                pair += 1


def own_kernel(
    both_ref, mine_ref, w_own_hbm, w_other_ref, query_ref, acc_ref, stats_ref, w_own_ref, sems
):
    count = both_ref.shape[0]
    copies = [
        pltpu.make_async_copy(w_own_hbm.at[i], w_own_ref.at[i], sems.at[i]) for i in range(3)
    ]
    for copy in copies:
        copy.start()
    both = both_ref[...]
    pairs = acc_ref.shape[0] // LANES
    per_step = STEP_COLS // LANES
    halves = ((w_other_ref, pairs // 2), (w_own_ref, 0))
    for weights, pair in halves:
        if weights is w_own_ref:
            copies[0].wait()
        for start in range(0, weights.shape[2], STEP_COLS):
            queries_t = dot(both, weights[0, :, start : start + STEP_COLS]).astype(BF16).T
            for i in range(per_step):
                zero = jnp.zeros((HDIM, count), BF16)
                row = i * LANES
                query_ref[pair, :HDIM, :count] = queries_t[row : row + HDIM]
                query_ref[pair, :HDIM, count:] = zero
                query_ref[pair, HDIM:, :count] = zero
                query_ref[pair, HDIM:, count:] = queries_t[row + HDIM : row + LANES]
                pair += 1
    copies[1].wait()
    copies[2].wait()
    attend_rows(mine_ref[...], (w_own_ref, w_other_ref), query_ref, acc_ref, stats_ref, True)


def own_attention(both, mine, w_own, w_other):
    count, width = both.shape
    pairs = width // LANES
    return pl.pallas_call(
        own_kernel,
        in_specs=[in_vmem(), in_vmem(), pl.BlockSpec(memory_space=pl.ANY), in_vmem()],
        out_specs=[in_vmem()] * 4,
        out_shape=[
            vmem_out((pairs, LANES, 2 * count), BF16),
            vmem_out((width, count), F32),
            vmem_out((pairs, 8, 2 * count), F32),
            vmem_out(w_own.shape, BF16),
        ],
        scratch_shapes=[pltpu.SemaphoreType.DMA((3,))],
        compiler_params=params(6),
        name="own_attention",
    )(held(both), held(mine), in_hbm(w_own), held(w_other))


def block_kernel(*refs, distances, loads):
    near = len(distances)
    here_ref, core_ref, mask_ref, query_ref, w_own_ref, w_other_ref = refs[:6]
    rows_refs = refs[6 : 6 + near]
    sources = refs[6 + near : 6 + near + loads]
    acc_ref, stats_ref = refs[8 + near + loads : 10 + near + loads]
    targets = refs[10 + near + loads : 10 + near + 2 * loads]
    sems = refs[10 + near + 2 * loads]
    copies = [
        pltpu.make_async_copy(source, target, sems.at[i])
        for i, (source, target) in enumerate(zip(sources, targets))
    ]
    for copy in copies:
        copy.start()
    here = here_ref[0]
    blocks = mask_ref.shape[1]
    for distance, rows_ref in zip(distances, rows_refs):
        source = jnp.where(core_ref[0] == 0, here - distance, here + distance)
        inside = (source >= 0) & (source < blocks)
        listed = mask_ref[here % 8, jnp.clip(source, 0, blocks - 1)]

        @pl.when(inside & (listed > 0))
        def _(rows_ref=rows_ref):
            attend_rows(
                rows_ref[...], (w_own_ref, w_other_ref), query_ref, acc_ref, stats_ref, False
            )

    for copy in copies:
        copy.wait()


def block_attention(place, block_mask, queries, w_own, w_other, near, acc, stats, loaded):
    blocks = block_mask.shape[0]
    distances = tuple(d for d, _ in near)
    count = len(near)
    loads = len(loaded)

    def body(*refs):
        block_kernel(*refs, distances=distances, loads=loads)

    grid_spec = pltpu.PrefetchScalarGridSpec(
        num_scalar_prefetch=2,
        grid=(1,),
        in_specs=[
            pl.BlockSpec((8, blocks), lambda j, s, c: (s[0] // 8, 0), memory_space=pltpu.SMEM),
        ]
        + [in_vmem()] * (3 + count)
        + [pl.BlockSpec(memory_space=pl.ANY)] * loads
        + [in_vmem()] * 2,
        out_specs=[in_vmem()] * (2 + loads),
        scratch_shapes=[pltpu.SemaphoreType.DMA((loads,))],
    )
    at = 6 + count + loads
    outs = pl.pallas_call(
        body,
        grid_spec=grid_spec,
        out_shape=[vmem_out(acc.shape, F32), vmem_out(stats.shape, F32)]
        + [vmem_out(array.shape, BF16) for array in loaded],
        input_output_aliases={at: 0, at + 1: 1},
        compiler_params=params(6),
        name="block_attention",
    )(
        *place,
        block_mask,
        held(queries),
        held(w_own),
        held(w_other),
        *[held(rows) for _, rows in near],
        *[in_hbm(array) for array in loaded],
        held(acc),
        held(stats),
    )
    return outs[0], outs[1], outs[2:]


def pack_kernel(here_ref, core_ref, acc_ref, stats_ref, out_ref, keep_ref, level_ref, log_ref):
    half = out_ref.shape[1]
    count = 2 * half
    width = acc_ref.shape[0]
    pairs = stats_ref.shape[0]
    mine = core_ref[0]
    away = pl.ds(pl.multiple_of((1 - mine) * half, half), half)
    near = pl.ds(pl.multiple_of(mine * half, half), half)
    row = width
    for pair in range(pairs):
        for head in range(2):
            rows = slice((2 * pair + head) * HDIM, (2 * pair + head + 1) * HDIM)
            lanes = slice(head * count, (head + 1) * count)
            total = stats_ref[pair, 1:2, lanes]
            log_ref[0:1, :] = stats_ref[pair, 0:1, lanes] * EXP_SCALE + jnp.log2(total)
            log_ref[1:2, :] = 1.0 / total
            keep_ref[rows, :] = acc_ref[rows, near] * log_ref[1:2, near]
            level_ref[2 * pair + head : 2 * pair + head + 1, :] = log_ref[0:1, near]
            level = log_ref[0:1, away]
            out_ref[rows, :] = (acc_ref[rows, away] * log_ref[1:2, away]).astype(BF16)
            first = level.astype(BF16).astype(F32)
            second = (level - first).astype(BF16).astype(F32)
            third = level - first - second
            pieces = jnp.concatenate([first, second, third, jnp.zeros((13, half), F32)], axis=0)
            out_ref[row : row + 16, :] = pieces.astype(BF16)
            row += 16


def pack(place, acc, stats):
    width, count = acc.shape
    half = count // 2
    heads = 2 * stats.shape[0]
    rows = width + 16 * heads
    grid_spec = pltpu.PrefetchScalarGridSpec(
        num_scalar_prefetch=2,
        grid=(1,),
        in_specs=[in_vmem()] * 2,
        out_specs=[
            pl.BlockSpec((rows, half), lambda i, s, c: (0, 0)),
            pl.BlockSpec((width, half), lambda i, s, c: (0, 0)),
            pl.BlockSpec((heads, half), lambda i, s, c: (0, 0)),
        ],
        scratch_shapes=[pltpu.VMEM((8, count), F32)],
    )
    return pl.pallas_call(
        pack_kernel,
        grid_spec=grid_spec,
        out_shape=[
            jax.ShapeDtypeStruct((rows, half), BF16),
            jax.ShapeDtypeStruct((width, half), F32),
            jax.ShapeDtypeStruct((heads, half), F32),
        ],
        compiler_params=params(6),
        name="pack",
    )(*place, held(acc), held(stats))


def tail_kernel(
    here_ref,
    core_ref,
    sent_ref,
    keep_ref,
    level_ref,
    tokens_ref,
    gain_ref,
    bias_ref,
    w_out_own,
    w_out_other,
    w_up_own,
    w_up_other,
    w_down_own,
    w_down_other,
    out_ref,
):
    _, width = tokens_ref.shape
    heads = level_ref.shape[0]
    pieces = []
    for head in range(heads):
        other = (head + heads // 2) % heads
        rows = slice(head * HDIM, (head + 1) * HDIM)
        other_rows = slice(other * HDIM, (other + 1) * HDIM)
        level = level_ref[head : head + 1, :]
        base = width + 16 * other
        sent = sent_ref[base : base + 16, :].astype(F32)
        their_level = sent[0:1] + sent[1:2] + sent[2:3]
        top = jnp.maximum(level, their_level)
        my_part = jnp.exp2(level - top)
        their_part = jnp.exp2(their_level - top)
        scale = 1.0 / (my_part + their_part)
        merged = keep_ref[rows, :] * (my_part * scale)
        merged = merged + sent_ref[other_rows, :].astype(F32) * (their_part * scale)
        pieces.append(merged.astype(BF16))
    attended = jnp.concatenate(pieces, axis=0).T
    halfway = width // 2
    projected = dot(attended[:, :halfway], w_out_own[...]) + dot(
        attended[:, halfway:], w_out_other[...]
    )
    resid = (tokens_ref[...].astype(F32) + projected).astype(BF16)
    normed = layer_norm(resid, gain_ref[...], bias_ref[...]).astype(BF16)
    total = resid.astype(F32)
    chunk = 512
    for up, down in ((w_up_own, w_down_own), (w_up_other, w_down_other)):
        for start in range(0, up.shape[1], chunk):
            raised = dot(normed, up[:, start : start + chunk])
            hidden = (raised * (1.0 + lax.erf(raised * (0.5**0.5))) * 0.5).astype(BF16)
            total = total + dot(hidden, down[start : start + chunk, :])
    out_ref[...] = total.astype(BF16)


def tail(place, sent, keep, level, tokens, gain, bias, weights):
    rows, width = tokens.shape
    sent_rows = sent.shape[0] // 2
    vector = pl.BlockSpec((1, width), lambda i, s, c: (0, 0))
    grid_spec = pltpu.PrefetchScalarGridSpec(
        num_scalar_prefetch=2,
        grid=(1,),
        in_specs=[
            pl.BlockSpec((sent_rows, rows), lambda i, s, c: (1 - c[0], 0)),
            pl.BlockSpec(keep.shape, lambda i, s, c: (0, 0)),
            pl.BlockSpec(level.shape, lambda i, s, c: (0, 0)),
            pl.BlockSpec((rows, width), lambda i, s, c: (0, 0)),
            vector,
            vector,
        ]
        + [in_vmem()] * len(weights),
        out_specs=pl.BlockSpec((rows, width), lambda i, s, c: (0, 0)),
    )
    return pl.pallas_call(
        tail_kernel,
        grid_spec=grid_spec,
        out_shape=jax.ShapeDtypeStruct(tokens.shape, BF16),
        compiler_params=params(8),
        name="tail",
    )(
        *place,
        sent,
        keep,
        level,
        tokens,
        gain.reshape(1, -1),
        bias.reshape(1, -1),
        *[held(weight) for weight in weights],
    )


def from_partner(array):
    return lax.ppermute(array, "head", [(0, 1), (1, 0)])


def from_block(array, distance):
    blocks = lax.axis_size("seq")
    ahead = [(2 * i, 2 * (i + distance)) for i in range(blocks - distance)]
    behind = [(2 * i + 1, 2 * (i - distance) + 1) for i in range(distance, blocks)]
    return lax.ppermute(array, ("seq", "head"), ahead + behind)


def shards(tokens, ln1_gain, ln1_bias, w_qkv, w_out, ln2_gain, ln2_bias, w_up, w_down, block_mask):
    here = lax.axis_index("seq")
    core = lax.axis_index("head")
    place = (here.astype(jnp.int32).reshape(1), core.astype(jnp.int32).reshape(1))
    w_own = jnp.transpose(w_qkv, (1, 0, 2))
    mine = norm_rows(place, tokens, ln1_gain, ln1_bias)
    both = lax.all_gather(mine, "head", axis=0, tiled=True)
    near = {}
    for d in range(1, REACH + 1):
        near[d] = from_block(both, d)
    w_other = from_partner(w_own)
    w_out_other = from_partner(w_out)
    w_up_other = from_partner(w_up)
    w_down_other = from_partner(w_down)
    queries, acc, stats, w_kept = own_attention(both, mine, w_own, w_other)
    loads = ((w_out, w_up, w_down), (w_out_other, w_up_other, w_down_other))
    weights = []
    for part, distances in enumerate(BLOCK_ORDER):
        acc, stats, loaded = block_attention(
            place,
            block_mask,
            queries,
            w_kept,
            w_other,
            [(d, near[d]) for d in distances],
            acc,
            stats,
            loads[part],
        )
        weights.append(loaded)
    packed, keep, level = pack(place, acc, stats)
    sent = lax.all_gather(packed, "head", axis=0, tiled=True)
    ordered = [weight for both_halves in zip(*weights) for weight in both_halves]
    return tail(place, sent, keep, level, tokens, ln2_gain, ln2_bias, ordered)


BLOCK_ORDER = ((1, 3), (4, 2))


def solution(mesh):
    in_specs = (
        P(("seq", "head"), None),
        P(),
        P(),
        P(None, None, "head"),
        P("head", None),
        P(),
        P(),
        P(None, "head"),
        P("head", None),
        P(),
    )
    out_specs = P(("seq", "head"), None)
    return jax.shard_map(
        shards, mesh=mesh, in_specs=in_specs, out_specs=out_specs, check_vma=False
    )
```
